32 devices in a mesh: grp: 2 (over x), feat: 16 (over z, y, core).
Axes of the slice: x: 2, y: 2, z: 4, core: 2. Of those that a mesh axis runs over, the one named last changes fastest.
Arguments:
- x_acts: bfloat16 [8, 1024, 4096], P('grp'), parts along dimension 0, may hold values from -6 to 6
- delta: bfloat16 [8, 1024, 4096], P('grp', None, 'feat'), parts along dimension 0, may hold values from -6 to 6
- pattern: int32 [32, 32], replicated, may hold values 0 or 1
- row_signs: int32 [4096], replicated, may hold values from -1 to 1, as said below
- col_signs: int32 [4096], replicated, may hold values from -1 to 1, as said below
- cols: int32 [8192], replicated, may hold values from 0 to 16777215
Outputs:
- sketch: float32 [8, 8192], P('grp'), parts along dimension 0
The draws below stay inside these ranges and needn't reach their ends.
There are 2 independent parts, one for each index of `grp`. The reference program is written for one: setup_inputs(seed, part) draws one part's arguments, and reference() takes and returns one part's arrays. A program takes and returns all parts, laid end to end along the dimension named above; an argument that names none is the same for every part. Nothing has to cross between parts.
Inputs may be any that keep to these rules, and one draw needn't show every extreme that they name: `row_signs`: every entry is -1 or +1. `col_signs`: every entry is -1 or +1.
All inputs are finite; a program needn't handle non-finite values.
Results may differ from the reference program's by a relative error of at most 0.0029.
Values may be sent and summed in bfloat16 or wider, within the bound.
No kernel may reach another device: no remote copies, remote signals or barrier semaphores. Data moves between devices by JAX's collectives and lax.ppermute only.
A program may use at most 192 MiB of HBM per device.

```python
import math
import jax
import jax.numpy as jnp
from jax import lax

D_IN = 4096
D_OUT = 4096
BLK = 128
SKETCH = 8192
EX = 4
TOK = 1024


def draw_row_signs(key, part):
    coin_bits = jax.random.randint(jax.random.fold_in(key, 11), (D_OUT,), 0, 2)
    return (2 * coin_bits - 1).astype(jnp.int32)


def draw_col_signs(key, part):
    coin_bits = jax.random.randint(jax.random.fold_in(key, 23), (D_IN,), 0, 2)
    return (2 * coin_bits - 1).astype(jnp.int32)


def plant(array, stream_key, least, largest):
    longest = array.shape.index(max(array.shape))
    spots = []
    for shift in (0, 1):
        where = [jax.random.randint(jax.random.fold_in(stream_key, axis), (), 0, length) for axis, length in enumerate(array.shape)]
        where[longest] = (where[longest] + shift) % array.shape[longest]
        spots.append(tuple(where))
    return array.at[spots[0]].set(least).at[spots[1]].set(largest)


def steps_of(stream_key, dims, split, smallest, high):
    loudness, own = 1.0, jax.random.fold_in(stream_key, 6)
    for position, shards_of in split:
        heights = jnp.exp(jax.random.uniform(jax.random.fold_in(own, position), (shards_of,), jnp.float32, smallest / len(split), high / len(split)))
        loudness = loudness * jnp.repeat(heights, dims[position] // shards_of).reshape([-1 if axis == position else 1 for axis in range(len(dims))])
    return loudness


def normal_values(own_key, extent, width, reach, split=(), dtype=jnp.bfloat16):
    result = jax.random.normal(own_key, extent, jnp.float32) * width
    if len(split) > 0:
        result = steps_of(own_key, extent, split, -0.22, 0.18) * result
    return jnp.clip(result, min=-reach, max=reach).astype(dtype)


def setup_inputs(seed: int = 0, part: int = 0) -> dict:
    streams_of = jax.random.split(jax.random.key(seed), 7)
    part_splits = jax.random.split(jax.random.fold_in(streams_of[6], part), 7)
    x_acts = normal_values(part_splits[0], (EX, TOK, D_IN), 1.0, 6.0)
    delta = normal_values(part_splits[1], (EX, TOK, D_OUT), 1.0, 6.0, ((2, 16),))
    pattern = plant((jax.random.randint(streams_of[2], (D_OUT // BLK, D_IN // BLK), 0, 2) < 1).astype(jnp.int32), jax.random.fold_in(streams_of[2], 1), 0, 1)
    row_signs = draw_row_signs(jax.random.fold_in(streams_of[6], 71), part)
    col_signs = draw_col_signs(jax.random.fold_in(streams_of[6], 71), part)
    cols = plant(jax.random.randint(streams_of[5], (SKETCH,), 0, D_OUT * D_IN), jax.random.fold_in(streams_of[5], 1), 0, (D_OUT * D_IN) - 1).astype(jnp.int32)
    return dict(x_acts=x_acts, delta=delta, pattern=pattern, row_signs=row_signs, col_signs=col_signs, cols=cols)


def walsh_transform(values, axis_pos):
    values = jnp.moveaxis(values, axis_pos, -1)
    length = values.shape[-1]
    leading = values.shape[:-1]
    half_len = 1
    while half_len < length:
        blocks = values.reshape(leading + (length // (2 * half_len), 2, half_len))
        lower = blocks[..., 0, :]
        upper = blocks[..., 1, :]
        values = jnp.stack([lower + upper, lower - upper], axis=-2).reshape(leading + (length,))
        half_len = half_len * 2
    return jnp.moveaxis(values, -1, axis_pos)

def reference(x_acts, delta, pattern, row_signs, col_signs, cols):
    block_mask = jnp.repeat(jnp.repeat(pattern, BLK, axis=0), BLK, axis=1).astype(jnp.float32)
    sign_values = (row_signs[:, None] * col_signs[None, :]).astype(jnp.float32)

    def one_example(inputs):
        acts_one, delta_one = inputs
        gradient = jnp.dot(delta_one.T, acts_one, preferred_element_type=jnp.float32) / TOK
        gradient = (gradient * block_mask).astype(jnp.bfloat16)
        signed = gradient.astype(jnp.float32) * sign_values
        transformed = walsh_transform(walsh_transform(signed, 1), 0)
        return transformed.reshape(-1)[cols] / math.sqrt(SKETCH)
    return lax.map(one_example, (x_acts, delta))
```

```python
import functools
import math

import jax
import jax.numpy as jnp
from jax import lax
from jax.experimental import pallas as pl
from jax.experimental.pallas import tpu as pltpu
from jax.sharding import PartitionSpec as P

BLK = 128
LANES = 128
SUBLANES = 8
CHUNK = 1024
VMEM_LIMIT = 60 * 2**20


def partner(value, axis, apart):
    mask = 2**apart
    pairs = [(source, source ^ mask) for source in range(lax.axis_size(axis))]
    return lax.ppermute(value, axis, pairs)


def parity(ids):
    for shift in (8, 4, 2, 1):
        ids = ids ^ (ids >> shift)
    return ids & 1


def transform_kernel(
    examples, free, n_blocks, tile_idx, sign_idx, x_ref, d_ref, factor_ref,
    mask_ref, rows_ref, out_ref, dt_ref, had_ref, sign_ref, s_ref, t_ref,
):
    example, chunk = pl.program_id(0), pl.program_id(1)
    last = (example == pl.num_programs(0) - 1) & (chunk == pl.num_programs(1) - 1)
    rows = d_ref.shape[2]
    width = x_ref.shape[2]
    blocks_here = width // LANES
    n_low = n_blocks // free
    row_blocks = mask_ref.shape[0]
    band = rows // row_blocks

    @pl.when((example == 0) & (chunk == 0))
    def _():
        left = lax.broadcasted_iota(jnp.int32, (rows, rows), 0)
        right = lax.broadcasted_iota(jnp.int32, (rows, rows), 1)
        had_ref[...] = (1 - 2 * parity(left & right)).astype(jnp.bfloat16)

        def signs(step, carry):
            base = step * (SUBLANES * SUBLANES)
            shape = (SUBLANES * SUBLANES, LANES)
            row = base + lax.broadcasted_iota(jnp.int32, shape, 0)
            lane = lax.broadcasted_iota(jnp.int32, shape, 1)
            entry = row // SUBLANES
            bit = row % SUBLANES // examples
            both = (entry % LANES & lane) ^ ((entry // LANES & bit) << 7)
            sign_ref[pl.ds(pl.multiple_of(base, SUBLANES * SUBLANES), shape[0]), :] = (
                1 - 2 * parity(both)
            ).astype(jnp.float32)
            return carry

        lax.fori_loop(0, free * LANES // SUBLANES, signs, 0)

    @pl.when(chunk == 0)
    def _():
        dt_ref[...] = (d_ref[0] * rows_ref[...]).T

    grad = jnp.dot(dt_ref[...], x_ref[0], preferred_element_type=jnp.float32)
    for b in range(row_blocks):
        part = slice(b * band, (b + 1) * band)
        s_ref[part, :] = (grad[part, :] * mask_ref[b : b + 1, :]).astype(jnp.bfloat16)
    out = jnp.dot(had_ref[...], s_ref[...], preferred_element_type=jnp.float32)
    for j in range(blocks_here):
        block = chunk * blocks_here + j
        start = (block % n_low) * rows * SUBLANES + block // n_low * examples + example
        t_ref[pl.ds(start, rows, stride=SUBLANES), :] = out[:, j * LANES : (j + 1) * LANES]

    @pl.when(last)
    def _():
        def butterfly(row, carry):
            tiles = [
                t_ref[pl.ds(pl.multiple_of((q * rows + row) * SUBLANES, SUBLANES), SUBLANES), :]
                for q in range(n_low)
            ]
            half = 1
            while half < n_low:
                tiles = [
                    tiles[q] + tiles[q + half] if q & half == 0 else tiles[q - half] - tiles[q]
                    for q in range(n_low)
                ]
                half *= 2
            for q in range(n_low):
                t_ref[pl.ds(pl.multiple_of((q * rows + row) * SUBLANES, SUBLANES), SUBLANES), :] = tiles[q]
            return carry

        lax.fori_loop(0, rows, butterfly, 0, unroll=2)

        lane = lax.broadcasted_iota(jnp.int32, (SUBLANES, LANES), 1)

        def term(group, first, count):
            if count == 1:
                k = group * LANES + first
                tile = pl.multiple_of(tile_idx[k], SUBLANES)
                sign = pl.multiple_of(sign_idx[k], SUBLANES)
                return t_ref[pl.ds(tile, SUBLANES), :] * sign_ref[pl.ds(sign, SUBLANES), :]
            half = count // 2
            left, right = term(group, first, half), term(group, first + half, half)
            low = lane & half == 0
            return jnp.where(low, left, right) + pltpu.roll(
                jnp.where(low, right, left), half, 1
            )

        def sample(group, carry):
            found = term(group, 0, LANES)
            total = found[:examples]
            for bit in range(1, free):
                total = total + found[bit * examples : (bit + 1) * examples]
            here = pl.ds(pl.multiple_of(group * LANES, LANES), LANES)
            out_ref[:, here] = total * factor_ref[pl.ds(group, 1), :]
            return carry

        lax.fori_loop(0, out_ref.shape[1] // LANES, sample, 0)


def transform(x_acts, delta, factor, mask, sign_rows, tile_idx, sign_idx):
    examples, tokens, width = x_acts.shape
    rows = delta.shape[2]
    n_kept = tile_idx.shape[0]
    free = SUBLANES // examples
    chunk = CHUNK
    whole = lambda shape: pl.BlockSpec(shape, lambda e, j, *_: (0,) * len(shape))
    kernel = functools.partial(transform_kernel, examples, free, width // LANES)
    return pl.pallas_call(
        kernel,
        out_shape=jax.ShapeDtypeStruct((examples, n_kept), jnp.float32),
        grid_spec=pltpu.PrefetchScalarGridSpec(
            num_scalar_prefetch=2,
            grid=(examples, width // chunk),
            in_specs=[
                pl.BlockSpec((1, tokens, chunk), lambda e, j, *_: (e, 0, j)),
                pl.BlockSpec((1, tokens, rows), lambda e, j, *_: (e, 0, 0)),
                whole(factor.shape),
                pl.BlockSpec((mask.shape[0], chunk), lambda e, j, *_: (0, j)),
                whole(sign_rows.shape),
            ],
            out_specs=whole((examples, n_kept)),
            scratch_shapes=[
                pltpu.VMEM((rows, tokens), jnp.bfloat16),
                pltpu.VMEM((rows, rows), jnp.bfloat16),
                pltpu.VMEM((free * LANES * SUBLANES, LANES), jnp.float32),
                pltpu.VMEM((rows, chunk), jnp.bfloat16),
                pltpu.VMEM((rows * width // LANES * examples, LANES), jnp.float32),
            ],
        ),
        compiler_params=pltpu.CompilerParams(vmem_limit_bytes=VMEM_LIMIT),
    )(tile_idx, sign_idx, x_acts, delta, factor, mask, sign_rows)


def per_device(x_acts, delta, pattern, row_signs, col_signs, cols):
    examples, tokens, width_in = x_acts.shape
    rows = delta.shape[2]
    n_kept = cols.shape[0]
    free = SUBLANES // examples
    n_low = width_in // LANES // free
    feat = lax.axis_size("feat")
    me = lax.axis_index("feat")

    first_row = me * rows
    row_blocks = max(rows // BLK, 1)
    here = lax.dynamic_slice_in_dim(pattern, first_row // BLK, row_blocks, 0)
    mask = (jnp.repeat(here, BLK, axis=1) * col_signs[None]).astype(jnp.float32)
    sign_rows = lax.dynamic_slice_in_dim(row_signs, first_row, rows, 0)
    sign_rows = sign_rows[None].astype(jnp.bfloat16)

    kept_row, kept_col = cols // width_in, cols % width_in
    block, lane = kept_col // LANES, kept_col % LANES
    tile_idx = (block % n_low * rows + kept_row % rows) * SUBLANES
    sign_idx = (block // n_low * LANES + lane) * SUBLANES
    factor = (1 - 2 * parity(kept_row // rows & me)).astype(jnp.float32)
    factor = (factor / (tokens * math.sqrt(n_kept))).reshape(n_kept // LANES, LANES)

    value = transform(x_acts, delta, factor, mask, sign_rows, tile_idx, sign_idx)

    bits = max(feat - 1, 0).bit_length()
    half = n_kept // 2
    low = me % 2 == 0
    mine = jnp.where(low, value[:, :half], value[:, half:])
    other = jnp.where(low, value[:, half:], value[:, :half])
    mine = mine + partner(other, "feat", 0)
    for bit in range(1, bits):
        mine = mine + partner(mine, "feat", bit)
    back = partner(mine, "feat", 0)
    return jnp.concatenate([jnp.where(low, mine, back), jnp.where(low, back, mine)], axis=1)


def solution(mesh):
    placed = (P("grp", None, None), P("grp", None, "feat"), P(), P(), P(), P())
    return jax.shard_map(
        per_device, mesh=mesh, in_specs=placed, out_specs=P("grp", None), check_vma=False
    )
```

```python
import functools
import math

import jax
import jax.numpy as jnp
from jax import lax
from jax.experimental import pallas as pl
from jax.experimental.pallas import tpu as pltpu
from jax.sharding import PartitionSpec as P

BLK = 128
LANES = 128
SUBLANES = 8
AT_ONCE = 8
PARTS = 4
PAD = 8
VMEM_LIMIT = 62 * 2**20


def partner(value, axis, apart):
    mask = 2**apart
    pairs = [(source, source ^ mask) for source in range(lax.axis_size(axis))]
    return lax.ppermute(value, axis, pairs)


def parity(ids):
    for shift in (8, 4, 2, 1):
        ids = ids ^ (ids >> shift)
    return ids & 1


def iota(shape, dim):
    return lax.broadcasted_iota(jnp.int32, shape, dim)


def aligned(index, unit):
    return pl.multiple_of(index * unit, unit)


def butterfly(tiles):
    half = 1
    while half < len(tiles):
        tiles = [
            tiles[q] + tiles[q + half] if q & half == 0 else tiles[q - half] - tiles[q]
            for q in range(len(tiles))
        ]
        half *= 2
    return tiles


def sketch_kernel(
    scale, pattern, x_hbm, d_hbm, cols_ref, rows_ref, signs_ref, mine_ref, other_ref,
    x_ref, d_ref, dt_ref, had_ref, flip_ref, idx_ref, t_ref, x_sem, d_sem, idx_sem,
    idx_smem, listed,
):
    examples, tokens, width = x_hbm.shape
    rows = d_hbm.shape[2]
    n_cols = width // LANES
    bands = dt_ref.shape[0] // examples
    band = rows // bands
    n_blocks = bands * n_cols
    block_rows = band * examples
    n_kept = cols_ref.shape[0] * LANES
    per_vreg = SUBLANES // examples
    me = lax.axis_index("feat")
    step = tokens // PARTS

    def x_copy(example, part):
        where = pl.ds(part * step, step)
        slot = example % 2
        return pltpu.make_async_copy(
            x_hbm.at[example, where], x_ref.at[slot, where], x_sem.at[slot, part]
        )

    d_copy = pltpu.make_async_copy(d_hbm, d_ref, d_sem)
    d_copy.start()
    for example in range(min(2, examples)):
        for part in range(PARTS):
            x_copy(example, part).start()

    cols = cols_ref[...]
    kept_row, kept_col = cols // width, cols % width
    local = kept_row % rows
    block = local // band * n_cols + kept_col // LANES
    place = iota(cols.shape, 0) % per_vreg
    idx_ref[...] = PAD + (block * band + local % band) * examples - place * examples

    had_ref[...] = (1 - 2 * parity(iota((band, band), 0) & iota((band, band), 1))).astype(
        jnp.bfloat16
    )
    bits = (iota((SUBLANES, LANES), 1) >> iota((SUBLANES, LANES), 0) & 1).astype(jnp.bfloat16)

    def flips(group, carry):
        lane = cols_ref[pl.ds(group, 1), :] % LANES
        mine = (lane >> iota((SUBLANES, LANES), 0) & 1).astype(jnp.bfloat16)
        shared = lax.dot_general(
            mine, bits, (((0,), (0,)), ((), ())), preferred_element_type=jnp.float32
        )
        odd = (shared.astype(jnp.int32) & 1).astype(jnp.float32)
        flip_ref[pl.ds(aligned(group, LANES), LANES), :] = 1.0 - 2.0 * odd
        return carry

    lax.fori_loop(0, n_kept // LANES, flips, 0)

    idx_copy = pltpu.make_async_copy(idx_ref, idx_smem, idx_sem)
    idx_copy.start()

    first = me * rows // BLK

    def listing(b, count):
        def one(q, count):
            listed[count] = b * n_cols + q
            return count + pattern[first + b, q]

        count = lax.fori_loop(0, n_cols, one, count)
        listed[count] = n_blocks
        return count + count % 2

    count = 0
    for b in range(bands):
        count = listing(b, count)
    for extra in range(AT_ONCE):
        listed[count + extra] = n_blocks
    n_steps = (count + AT_ONCE - 1) // AT_ONCE

    def clear(i, carry):
        @pl.when(pattern[first + i // n_cols, i % n_cols] == 0)
        def _():
            here = pl.ds(pl.multiple_of(PAD + i * block_rows, SUBLANES), block_rows)
            t_ref[here, :] = jnp.zeros((block_rows, LANES), jnp.float32)

        return carry

    lax.fori_loop(0, n_blocks, clear, 0)

    d_copy.wait()
    for example in range(examples):
        turned = (d_ref[example] * rows_ref[...]).T
        for b in range(bands):
            dt_ref[example * bands + b] = turned[b * band : (b + 1) * band, :]

    def one_example(example, carry):
        slot = example % 2
        for part in range(PARTS):
            x_copy(example, part).wait()

        def some_blocks(s, carry):
            ids = [listed[s * AT_ONCE + i] for i in range(AT_ONCE)]
            grads, signed, sums = [], [], []
            for i in range(0, AT_ONCE, 2):
                b = ids[i] // n_cols % bands
                acts = [
                    x_ref[slot, :, pl.ds(aligned(ids[i + k] % n_cols, LANES), LANES)]
                    for k in range(2)
                ]
                grads.append(
                    jnp.dot(
                        dt_ref[example * bands + b],
                        jnp.concatenate(acts, axis=1),
                        preferred_element_type=jnp.float32,
                    )
                )
            for i in range(0, AT_ONCE, 2):
                flip = jnp.concatenate(
                    [signs_ref[pl.ds(ids[i + k] % n_cols, 1), :] for k in range(2)], axis=1
                ).astype(jnp.float32)
                signed.append((grads[i // 2] * flip).astype(jnp.bfloat16))
            for i in range(0, AT_ONCE, 2):
                sums.append(
                    jnp.dot(had_ref[...], signed[i // 2], preferred_element_type=jnp.float32)
                )
            for i in range(AT_ONCE):
                start = PAD + ids[i] * block_rows + example
                half = slice(i % 2 * LANES, (i % 2 + 1) * LANES)
                t_ref[pl.ds(start, band, stride=examples), :] = sums[i // 2][:, half]
            return carry

        lax.fori_loop(0, n_steps, some_blocks, 0)

        @pl.when(example + 2 < examples)
        def _():
            for part in range(PARTS):
                x_copy(example + 2, part).start()

        return carry

    lax.fori_loop(0, examples, one_example, 0)

    def across(r, carry):
        def here(i):
            start = PAD + i * block_rows + r * SUBLANES
            return pl.ds(pl.multiple_of(start, SUBLANES), SUBLANES)

        for b in range(bands):
            tiles = butterfly([t_ref[here(b * n_cols + q), :] for q in range(n_cols)])
            if b % 2 == 0:
                for q in range(n_cols):
                    t_ref[here(b * n_cols + q), :] = tiles[q]
            else:
                for q in range(n_cols):
                    low = t_ref[here((b - 1) * n_cols + q), :]
                    t_ref[here((b - 1) * n_cols + q), :] = low + tiles[q]
                    t_ref[here(b * n_cols + q), :] = low - tiles[q]
        return carry

    lax.fori_loop(0, block_rows // SUBLANES, across, 0)

    idx_copy.wait()
    lane = iota((SUBLANES, LANES), 1)
    spot = iota((SUBLANES, LANES), 0) // examples
    n_groups = n_kept // LANES // per_vreg
    half = n_groups // 2

    def sample(out_ref, base):
        def body(i, carry):
            group = base + i
            found = jnp.zeros((SUBLANES, LANES), jnp.float32)
            for u in range(LANES):
                term = None
                for p in range(per_vreg):
                    line = group * per_vreg + p
                    tile = t_ref[pl.ds(idx_smem[line, u], SUBLANES), :]
                    flip = flip_ref[pl.ds(line * LANES + u, SUBLANES, stride=0), :]
                    tile = tile * flip
                    term = tile if p == 0 else jnp.where(spot == p, tile, term)
                total = jnp.sum(term, axis=1, keepdims=True)
                found = jnp.where(lane == u, total, found)
            for p in range(per_vreg):
                line = group * per_vreg + p
                top = cols_ref[pl.ds(line, 1), :] // width // rows
                factor = (1 - 2 * parity(top & me)).astype(jnp.float32) * scale
                there = pl.ds(aligned(i * per_vreg + p, LANES), LANES)
                out_ref[:, there] = found[p * examples : (p + 1) * examples] * factor
            return carry

        lax.fori_loop(0, half, body, 0)

    sample(other_ref, (1 - me % 2) * half)
    sample(mine_ref, me % 2 * half)


def sketch(x_acts, delta, pattern, sign_rows, col_signs, cols):
    examples, tokens, width = x_acts.shape
    rows = delta.shape[2]
    n_kept = cols.shape[0]
    bands = max(rows // BLK, 1)
    band = rows // bands
    n_blocks = bands * width // LANES
    hbm = pl.BlockSpec(memory_space=pl.ANY)
    vmem = pl.BlockSpec(memory_space=pltpu.VMEM)
    scale = 1.0 / (tokens * math.sqrt(n_kept))
    part = jax.ShapeDtypeStruct((examples, n_kept // 2), jnp.float32)
    return pl.pallas_call(
        functools.partial(sketch_kernel, scale),
        out_shape=(part, part),
        in_specs=[pl.BlockSpec(memory_space=pltpu.SMEM), hbm, hbm, vmem, vmem, vmem],
        out_specs=(vmem, vmem),
        scratch_shapes=[
            pltpu.VMEM((2, tokens, width), jnp.bfloat16),
            pltpu.VMEM((examples, tokens, rows), jnp.bfloat16),
            pltpu.VMEM((examples * bands, band, tokens), jnp.bfloat16),
            pltpu.VMEM((band, band), jnp.bfloat16),
            pltpu.VMEM((n_kept, LANES), jnp.float32),
            pltpu.VMEM((n_kept // LANES, LANES), jnp.int32),
            pltpu.VMEM((PAD + (n_blocks + 1) * band * examples, LANES), jnp.float32),
            pltpu.SemaphoreType.DMA((2, PARTS)),
            pltpu.SemaphoreType.DMA,
            pltpu.SemaphoreType.DMA,
            pltpu.SMEM((n_kept // LANES, LANES), jnp.int32),
            pltpu.SMEM((n_blocks + 2 * bands + AT_ONCE,), jnp.int32),
        ],
        compiler_params=pltpu.CompilerParams(vmem_limit_bytes=VMEM_LIMIT),
    )(
        pattern, x_acts, delta, cols.reshape(-1, LANES), sign_rows,
        col_signs.reshape(-1, LANES),
    )


def per_device(x_acts, delta, pattern, row_signs, col_signs, cols):
    rows = delta.shape[2]
    feat = lax.axis_size("feat")
    me = lax.axis_index("feat")
    sign_rows = lax.dynamic_slice_in_dim(row_signs, me * rows, rows, 0)
    sign_rows = sign_rows[None].astype(jnp.bfloat16)

    mine, other = sketch(x_acts, delta, pattern, sign_rows, col_signs, cols)

    bits = max(feat - 1, 0).bit_length()
    mine = mine + partner(other, "feat", 0)
    for bit in range(1, bits):
        mine = mine + partner(mine, "feat", bit)
    back = partner(mine, "feat", 0)
    low = me % 2 == 0
    return jnp.concatenate([jnp.where(low, mine, back), jnp.where(low, back, mine)], axis=1)


def solution(mesh):
    placed = (P("grp", None, None), P("grp", None, "feat"), P(), P(), P(), P())
    return jax.shard_map(
        per_device, mesh=mesh, in_specs=placed, out_specs=P("grp", None), check_vma=False
    )
```

```python
import functools
import math

import jax
import jax.numpy as jnp
from jax import lax
from jax.experimental import pallas as pl
from jax.experimental.pallas import tpu as pltpu
from jax.sharding import PartitionSpec as P

BLK = 128
LANES = 128
SUBLANES = 8
AT_ONCE = 8
GROUP = 4
PARTS = 4
PAD = 8
VMEM_LIMIT = 44 * 2**20


def partner(value, axis, apart):
    mask = 2**apart
    pairs = [(source, source ^ mask) for source in range(lax.axis_size(axis))]
    return lax.ppermute(value, axis, pairs)


def parity(ids):
    for shift in (8, 4, 2, 1):
        ids = ids ^ (ids >> shift)
    return ids & 1


def iota(shape, dim):
    return lax.broadcasted_iota(jnp.int32, shape, dim)


def aligned(index, unit):
    return pl.multiple_of(index * unit, unit)


def butterfly(tiles):
    half = 1
    while half < len(tiles):
        tiles = [
            tiles[q] + tiles[q + half] if q & half == 0 else tiles[q - half] - tiles[q]
            for q in range(len(tiles))
        ]
        half *= 2
    return tiles


def sketch_kernel(
    scale, pattern, x_hbm, d_hbm, cols_ref, rows_ref, signs_ref, mine_ref, other_ref,
    x_ref, d_ref, dt_ref, had_ref, flip_even, flip_odd, idx_ref, signed_ref, t_ref,
    x_sem, d_sem, idx_sem, idx_smem, listed,
):
    examples, tokens, width = x_hbm.shape
    rows = d_hbm.shape[2]
    n_cols = width // LANES
    bands = dt_ref.shape[0] // examples
    band = rows // bands
    n_blocks = bands * n_cols
    block_rows = band * examples
    n_kept = cols_ref.shape[0] * LANES
    per_vreg = SUBLANES // examples
    me = lax.axis_index("feat")
    step = tokens // PARTS

    def x_copy(example, part):
        where = pl.ds(part * step, step)
        slot = example % 2
        return pltpu.make_async_copy(
            x_hbm.at[example, where], x_ref.at[slot, where], x_sem.at[slot, part]
        )

    d_copy = pltpu.make_async_copy(d_hbm, d_ref, d_sem)
    d_copy.start()
    for example in range(min(2, examples)):
        for part in range(PARTS):
            x_copy(example, part).start()

    cols = cols_ref[...]
    kept_row, kept_col = cols // width, cols % width
    local = kept_row % rows
    block = local // band * n_cols + kept_col // LANES
    place = iota(cols.shape, 0) % per_vreg
    idx_ref[...] = PAD + (block * band + local % band) * examples - place * examples

    had_ref[...] = (1 - 2 * parity(iota((band, band), 0) & iota((band, band), 1))).astype(
        jnp.bfloat16
    )
    bits = (iota((SUBLANES, LANES), 1) >> iota((SUBLANES, LANES), 0) & 1).astype(jnp.bfloat16)

    def flips(group, flip_ref):
        digits = []
        for p in range(per_vreg):
            lane = cols_ref[pl.ds(group * per_vreg + p, 1), :] % LANES
            digits.append((lane >> iota((SUBLANES, LANES), 0) & 1).astype(jnp.bfloat16))
        shared = lax.dot_general(
            jnp.concatenate(digits, axis=1),
            bits,
            (((0,), (0,)), ((), ())),
            preferred_element_type=jnp.float32,
        )
        odd = (shared.astype(jnp.int32) & 1).astype(jnp.float32)
        flip_ref[...] = 1.0 - 2.0 * odd

    first = me * rows // BLK

    count = AT_ONCE
    for b in range(bands):
        for q in range(n_cols):
            listed[count] = b * n_cols + q
            count = count + pattern[first + b, q]
        for extra in range(GROUP):
            listed[count + extra] = n_blocks
        count = (count + GROUP - 1) // GROUP * GROUP
    for extra in range(AT_ONCE):
        listed[count + extra] = n_blocks
    n_steps = jnp.maximum((count - 1) // AT_ONCE, 1)
    for i in range(AT_ONCE):
        listed[i] = listed[n_steps * AT_ONCE + i]

    idx_copy = pltpu.make_async_copy(idx_ref, idx_smem, idx_sem)
    idx_copy.start()

    def clear(i, carry):
        @pl.when(pattern[first + i // n_cols, i % n_cols] == 0)
        def _():
            here = pl.ds(pl.multiple_of(PAD + i * block_rows, SUBLANES), block_rows)
            t_ref[here, :] = jnp.zeros((block_rows, LANES), jnp.float32)

        return carry

    lax.fori_loop(0, n_blocks, clear, 0)

    if rows % LANES == 0:
        row_flip = jnp.concatenate(
            [rows_ref[pl.ds(me * (rows // LANES) + i, 1), :] for i in range(rows // LANES)],
            axis=1,
        ).astype(jnp.bfloat16)
    else:
        row_flip = rows_ref[...].astype(jnp.bfloat16)
    d_copy.wait()
    for example in range(examples):
        turned = (d_ref[example] * row_flip).T
        for b in range(bands):
            dt_ref[example * bands + b] = turned[b * band : (b + 1) * band, :]

    def finish(at, example):
        sums = jnp.dot(had_ref[...], signed_ref[...], preferred_element_type=jnp.float32)
        for i in range(AT_ONCE):
            start = PAD + listed[at + i] * block_rows + example
            t_ref[pl.ds(start, band, stride=examples), :] = sums[:, i * LANES : (i + 1) * LANES]

    def one_example(example, carry):
        slot = example % 2
        for part in range(PARTS):
            x_copy(example, part).wait()

        def some_blocks(s, carry):
            finish(s * AT_ONCE, jnp.where(s == 0, jnp.maximum(example - 1, 0), example))
            for g in range(AT_ONCE // GROUP):
                ids = [listed[(s + 1) * AT_ONCE + g * GROUP + k] for k in range(GROUP)]
                acts = [
                    x_ref[slot, :, pl.ds(aligned(i % n_cols, LANES), LANES)] for i in ids
                ]
                flip = [signs_ref[pl.ds(i % n_cols, 1), :] for i in ids]
                grad = jnp.dot(
                    dt_ref[example * bands + ids[0] // n_cols % bands],
                    jnp.concatenate(acts, axis=1),
                    preferred_element_type=jnp.float32,
                )
                flip = jnp.concatenate(flip, axis=1).astype(jnp.float32)
                here = slice(g * GROUP * LANES, (g + 1) * GROUP * LANES)
                signed_ref[:, here] = (grad * flip).astype(jnp.bfloat16)
            return carry

        lax.fori_loop(0, n_steps, some_blocks, 0)

        @pl.when(example + 2 < examples)
        def _():
            for part in range(PARTS):
                x_copy(example + 2, part).start()

        return carry

    lax.fori_loop(0, examples, one_example, 0)
    finish(n_steps * AT_ONCE, examples - 1)

    def across(r, carry):
        def here(i):
            start = PAD + i * block_rows + r * SUBLANES
            return pl.ds(pl.multiple_of(start, SUBLANES), SUBLANES)

        for b in range(bands):
            tiles = butterfly([t_ref[here(b * n_cols + q), :] for q in range(n_cols)])
            if b % 2 == 0:
                for q in range(n_cols):
                    t_ref[here(b * n_cols + q), :] = tiles[q]
            else:
                for q in range(n_cols):
                    low = t_ref[here((b - 1) * n_cols + q), :]
                    t_ref[here((b - 1) * n_cols + q), :] = low + tiles[q]
                    t_ref[here(b * n_cols + q), :] = low - tiles[q]
        return carry

    lax.fori_loop(0, block_rows // SUBLANES, across, 0)

    idx_copy.wait()
    lane = iota((SUBLANES, LANES), 1)
    spot = iota((SUBLANES, LANES), 0) // examples
    n_groups = n_kept // LANES // per_vreg
    half = n_groups // 2

    def one_group(group, out_ref, at, flip_ref):
        found = jnp.zeros((SUBLANES, LANES), jnp.float32)
        for u in range(LANES):
            term = None
            for p in range(per_vreg):
                tile = t_ref[pl.ds(idx_smem[group * per_vreg + p, u], SUBLANES), :]
                tile = tile * flip_ref[pl.ds(p * LANES + u, SUBLANES, stride=0), :]
                term = tile if p == 0 else jnp.where(spot == p, tile, term)
            total = jnp.sum(term, axis=1, keepdims=True)
            found = jnp.where(lane == u, total, found)
        for p in range(per_vreg):
            top = cols_ref[pl.ds(group * per_vreg + p, 1), :] // width // rows
            factor = (1 - 2 * parity(top & me)).astype(jnp.float32) * scale
            there = pl.ds(aligned(at * per_vreg + p, LANES), LANES)
            out_ref[:, there] = found[p * examples : (p + 1) * examples] * factor

    def sample(out_ref, base):
        def body(i, carry):
            group = base + 2 * i
            flips(group + 1, flip_odd)
            one_group(group, out_ref, 2 * i, flip_even)
            flips(lax.rem(group + 2, n_groups), flip_even)
            one_group(group + 1, out_ref, 2 * i + 1, flip_odd)
            return carry

        lax.fori_loop(0, half // 2, body, 0)

    theirs = (1 - me % 2) * half
    flips(theirs, flip_even)
    sample(other_ref, theirs)
    sample(mine_ref, me % 2 * half)


def sketch(x_acts, delta, pattern, sign_rows, col_signs, cols):
    examples, tokens, width = x_acts.shape
    rows = delta.shape[2]
    n_kept = cols.shape[0]
    bands = max(rows // BLK, 1)
    band = rows // bands
    n_blocks = bands * width // LANES
    per_vreg = SUBLANES // examples
    hbm = pl.BlockSpec(memory_space=pl.ANY)
    vmem = pl.BlockSpec(memory_space=pltpu.VMEM)
    scale = 1.0 / (tokens * math.sqrt(n_kept))
    part = jax.ShapeDtypeStruct((examples, n_kept // 2), jnp.float32)
    return pl.pallas_call(
        functools.partial(sketch_kernel, scale),
        out_shape=(part, part),
        in_specs=[pl.BlockSpec(memory_space=pltpu.SMEM), hbm, hbm, vmem, vmem, vmem],
        out_specs=(vmem, vmem),
        scratch_shapes=[
            pltpu.VMEM((2, tokens, width), jnp.bfloat16),
            pltpu.VMEM((examples, tokens, rows), jnp.bfloat16),
            pltpu.VMEM((examples * bands, band, tokens), jnp.bfloat16),
            pltpu.VMEM((band, band), jnp.bfloat16),
            pltpu.VMEM((per_vreg * LANES, LANES), jnp.float32),
            pltpu.VMEM((per_vreg * LANES, LANES), jnp.float32),
            pltpu.VMEM((n_kept // LANES, LANES), jnp.int32),
            pltpu.VMEM((band, AT_ONCE * LANES), jnp.bfloat16),
            pltpu.VMEM((PAD + (n_blocks + 1) * band * examples, LANES), jnp.float32),
            pltpu.SemaphoreType.DMA((2, PARTS)),
            pltpu.SemaphoreType.DMA,
            pltpu.SemaphoreType.DMA,
            pltpu.SMEM((n_kept // LANES, LANES), jnp.int32),
            pltpu.SMEM((n_blocks + GROUP * bands + 2 * AT_ONCE,), jnp.int32),
        ],
        compiler_params=pltpu.CompilerParams(vmem_limit_bytes=VMEM_LIMIT),
    )(
        pattern, x_acts, delta, cols.reshape(-1, LANES), sign_rows,
        col_signs.reshape(-1, LANES),
    )


def per_device(x_acts, delta, pattern, row_signs, col_signs, cols):
    rows = delta.shape[2]
    feat = lax.axis_size("feat")
    me = lax.axis_index("feat")
    if rows % LANES == 0:
        sign_rows = row_signs.reshape(-1, LANES)
    else:
        sign_rows = lax.dynamic_slice_in_dim(row_signs, me * rows, rows, 0)[None]

    mine, other = sketch(x_acts, delta, pattern, sign_rows, col_signs, cols)

    bits = max(feat - 1, 0).bit_length()
    mine = mine + partner(other, "feat", 0)
    for bit in range(1, bits):
        mine = mine + partner(mine, "feat", bit)
    back = partner(mine, "feat", 0)
    low = me % 2 == 0
    return jnp.concatenate([jnp.where(low, mine, back), jnp.where(low, back, mine)], axis=1)


def solution(mesh):
    placed = (P("grp", None, None), P("grp", None, "feat"), P(), P(), P(), P())
    return jax.shard_map(
        per_device, mesh=mesh, in_specs=placed, out_specs=P("grp", None), check_vma=False
    )
```

```python
import functools
import math

import jax
import jax.numpy as jnp
from jax import lax
from jax.experimental import pallas as pl
from jax.experimental.pallas import tpu as pltpu
from jax.sharding import PartitionSpec as P

BLK = 128
LANES = 128
SUBLANES = 8
AT_ONCE = 8
GROUP = 4
PARTS = 4
PAD = 8
VMEM_LIMIT = 44 * 2**20


def partner(value, axis, apart):
    mask = 2**apart
    pairs = [(source, source ^ mask) for source in range(lax.axis_size(axis))]
    return lax.ppermute(value, axis, pairs)


def parity(ids):
    for shift in (8, 4, 2, 1):
        ids = ids ^ (ids >> shift)
    return ids & 1


def iota(shape, dim):
    return lax.broadcasted_iota(jnp.int32, shape, dim)


def aligned(index, unit):
    return pl.multiple_of(index * unit, unit)


def butterfly(tiles):
    half = 1
    while half < len(tiles):
        tiles = [
            tiles[q] + tiles[q + half] if q & half == 0 else tiles[q - half] - tiles[q]
            for q in range(len(tiles))
        ]
        half *= 2
    return tiles


def sketch_kernel(
    scale, pattern_hbm, x_hbm, d_hbm, cols_hbm, rows_hbm, signs_hbm, mine_ref, other_ref,
    pattern, cols_ref, rows_ref, signs_ref, small_sem, x_ref, d_ref, dt_ref, had_ref, flip_even, flip_odd, idx_ref, signed_ref, t_ref, x_sem, d_sem, idx_sem, idx_smem, listed,
):
    examples, tokens, width = x_hbm.shape
    rows = d_hbm.shape[2]
    n_cols = width // LANES
    bands = dt_ref.shape[0] // examples
    band = rows // bands
    n_blocks = bands * n_cols
    block_rows = band * examples
    n_kept = cols_ref.shape[0] * LANES
    per_vreg = SUBLANES // examples
    me = lax.axis_index("feat")
    step = tokens // PARTS

    def x_copy(example, part):
        where = pl.ds(part * step, step)
        slot = example % 2
        return pltpu.make_async_copy(
            x_hbm.at[example, where], x_ref.at[slot, where], x_sem.at[slot, part]
        )

    small = [
        pltpu.make_async_copy(source, target, small_sem.at[i])
        for i, (source, target) in enumerate(
            (
                (cols_hbm, cols_ref),
                (pattern_hbm, pattern),
                (rows_hbm, rows_ref),
                (signs_hbm, signs_ref),
            )
        )
    ]
    for copy in small:
        copy.start()
    d_copy = pltpu.make_async_copy(d_hbm, d_ref, d_sem)
    d_copy.start()
    for part in range(PARTS):
        x_copy(0, part).start()

    had_ref[...] = (1 - 2 * parity(iota((band, band), 0) & iota((band, band), 1))).astype(
        jnp.bfloat16
    )
    bits = (iota((SUBLANES, LANES), 1) >> iota((SUBLANES, LANES), 0) & 1).astype(jnp.bfloat16)
    for copy in small:
        copy.wait()

    cols = cols_ref[...]
    kept_row, kept_col = cols // width, cols % width
    local = kept_row % rows
    block = local // band * n_cols + kept_col // LANES
    place = iota(cols.shape, 0) % per_vreg
    idx_ref[...] = PAD + (block * band + local % band) * examples - place * examples

    def flips(group, flip_ref):
        digits = []
        for p in range(per_vreg):
            lane = cols_ref[pl.ds(group * per_vreg + p, 1), :] % LANES
            digits.append((lane >> iota((SUBLANES, LANES), 0) & 1).astype(jnp.bfloat16))
        shared = lax.dot_general(
            jnp.concatenate(digits, axis=1),
            bits,
            (((0,), (0,)), ((), ())),
            preferred_element_type=jnp.float32,
        )
        odd = (shared.astype(jnp.int32) & 1).astype(jnp.float32)
        flip_ref[...] = 1.0 - 2.0 * odd

    first = me * rows // BLK

    count = AT_ONCE
    for b in range(bands):
        for q in range(n_cols):
            listed[count] = b * n_cols + q
            count = count + pattern[first + b, q]
        for extra in range(GROUP):
            listed[count + extra] = n_blocks
        count = (count + GROUP - 1) // GROUP * GROUP
    for extra in range(AT_ONCE):
        listed[count + extra] = n_blocks
    n_steps = jnp.maximum((count - 1) // AT_ONCE, 1)
    for i in range(AT_ONCE):
        listed[i] = listed[n_steps * AT_ONCE + i]

    idx_copy = pltpu.make_async_copy(idx_ref, idx_smem, idx_sem)
    idx_copy.start()

    for b in range(bands):
        def clear(q, carry):
            @pl.when(pattern[first + b, q] == 0)
            def _():
                start = PAD + (b * n_cols + q) * block_rows
                here = pl.ds(pl.multiple_of(start, SUBLANES), block_rows)
                t_ref[here, :] = jnp.zeros((block_rows, LANES), jnp.float32)

            return carry

        lax.fori_loop(0, n_cols, clear, 0)

    if rows % LANES == 0:
        row_flip = jnp.concatenate(
            [rows_ref[pl.ds(me * (rows // LANES) + i, 1), :] for i in range(rows // LANES)],
            axis=1,
        ).astype(jnp.bfloat16)
    else:
        row_flip = rows_ref[...].astype(jnp.bfloat16)
    d_copy.wait()
    for example in range(examples):
        turned = (d_ref[example] * row_flip).T
        for b in range(bands):
            dt_ref[example * bands + b] = turned[b * band : (b + 1) * band, :]

    def finish(at, example):
        sums = jnp.dot(had_ref[...], signed_ref[...], preferred_element_type=jnp.float32)
        for i in range(AT_ONCE):
            start = PAD + listed[at + i] * block_rows + example
            t_ref[pl.ds(start, band, stride=examples), :] = sums[:, i * LANES : (i + 1) * LANES]

    def one_example(example, carry):
        for part in range(PARTS):
            x_copy(example, part).wait()

        @pl.when(example + 1 < examples)
        def _():
            for part in range(PARTS):
                x_copy(example + 1, part).start()


        def some_blocks(s, carry):
            finish(s * AT_ONCE, jnp.where(s == 0, jnp.maximum(example - 1, 0), example))
            for g in range(AT_ONCE // GROUP):
                ids = [listed[(s + 1) * AT_ONCE + g * GROUP + k] for k in range(GROUP)]
                acts = [
                    x_ref[example % 2, :, pl.ds(aligned(i % n_cols, LANES), LANES)] for i in ids
                ]
                flip = [signs_ref[pl.ds(i % n_cols, 1), :] for i in ids]
                grad = jnp.dot(
                    dt_ref[example * bands + ids[0] // n_cols % bands],
                    jnp.concatenate(acts, axis=1),
                    preferred_element_type=jnp.float32,
                )
                flip = jnp.concatenate(flip, axis=1).astype(jnp.float32)
                here = slice(g * GROUP * LANES, (g + 1) * GROUP * LANES)
                signed_ref[:, here] = (grad * flip).astype(jnp.bfloat16)
            return carry

        lax.fori_loop(0, n_steps, some_blocks, 0)

        return carry

    lax.fori_loop(0, examples, one_example, 0)
    finish(n_steps * AT_ONCE, examples - 1)

    def across(r, carry):
        def here(i):
            start = PAD + i * block_rows + r * SUBLANES
            return pl.ds(pl.multiple_of(start, SUBLANES), SUBLANES)

        for b in range(bands):
            tiles = butterfly([t_ref[here(b * n_cols + q), :] for q in range(n_cols)])
            if b % 2 == 0:
                for q in range(n_cols):
                    t_ref[here(b * n_cols + q), :] = tiles[q]
            else:
                for q in range(n_cols):
                    low = t_ref[here((b - 1) * n_cols + q), :]
                    t_ref[here((b - 1) * n_cols + q), :] = low + tiles[q]
                    t_ref[here(b * n_cols + q), :] = low - tiles[q]
        return carry

    lax.fori_loop(0, block_rows // SUBLANES, across, 0)

    idx_copy.wait()
    lane = iota((SUBLANES, LANES), 1)
    spot = iota((SUBLANES, LANES), 0) // examples
    n_groups = n_kept // LANES // per_vreg
    half = n_groups // 2

    def one_group(group, out_ref, at, flip_ref):
        found = jnp.zeros((SUBLANES, LANES), jnp.float32)
        for u in range(LANES):
            term = None
            for p in range(per_vreg):
                tile = t_ref[pl.ds(idx_smem[group * per_vreg + p, u], SUBLANES), :]
                tile = tile * flip_ref[pl.ds(p * LANES + u, SUBLANES, stride=0), :]
                term = tile if p == 0 else jnp.where(spot == p, tile, term)
            total = jnp.sum(term, axis=1, keepdims=True)
            found = jnp.where(lane == u, total, found)
        for p in range(per_vreg):
            top = cols_ref[pl.ds(group * per_vreg + p, 1), :] // width // rows
            factor = (1 - 2 * parity(top & me)).astype(jnp.float32) * scale
            there = pl.ds(aligned(at * per_vreg + p, LANES), LANES)
            out_ref[:, there] = found[p * examples : (p + 1) * examples] * factor

    def sample(out_ref, base):
        def body(i, carry):
            group = base + 2 * i
            flips(group + 1, flip_odd)
            one_group(group, out_ref, 2 * i, flip_even)
            flips(lax.rem(group + 2, n_groups), flip_even)
            one_group(group + 1, out_ref, 2 * i + 1, flip_odd)
            return carry

        lax.fori_loop(0, half // 2, body, 0)

    theirs = (1 - me % 2) * half
    flips(theirs, flip_even)
    sample(other_ref, theirs)
    sample(mine_ref, me % 2 * half)


def sketch(x_acts, delta, pattern, sign_rows, col_signs, cols):
    examples, tokens, width = x_acts.shape
    rows = delta.shape[2]
    n_kept = cols.shape[0]
    bands = max(rows // BLK, 1)
    band = rows // bands
    n_blocks = bands * width // LANES
    per_vreg = SUBLANES // examples
    hbm = pl.BlockSpec(memory_space=pltpu.HBM)
    vmem = pl.BlockSpec(memory_space=pltpu.VMEM)
    scale = 1.0 / (tokens * math.sqrt(n_kept))
    part = jax.ShapeDtypeStruct((examples, n_kept // 2), jnp.float32)
    return pl.pallas_call(
        functools.partial(sketch_kernel, scale),
        out_shape=(part, part),
        in_specs=[hbm] * 6,
        out_specs=(vmem, vmem),
        scratch_shapes=[
            pltpu.SMEM(pattern.shape, jnp.int32),
            pltpu.VMEM((n_kept // LANES, LANES), jnp.int32),
            pltpu.VMEM(sign_rows.shape, jnp.int32),
            pltpu.VMEM((width // LANES, LANES), jnp.int32),
            pltpu.SemaphoreType.DMA((4,)),
            pltpu.VMEM((2, tokens, width), jnp.bfloat16),
            pltpu.VMEM((examples, tokens, rows), jnp.bfloat16),
            pltpu.VMEM((examples * bands, band, tokens), jnp.bfloat16),
            pltpu.VMEM((band, band), jnp.bfloat16),
            pltpu.VMEM((per_vreg * LANES, LANES), jnp.float32),
            pltpu.VMEM((per_vreg * LANES, LANES), jnp.float32),
            pltpu.VMEM((n_kept // LANES, LANES), jnp.int32),
            pltpu.VMEM((band, AT_ONCE * LANES), jnp.bfloat16),
            pltpu.VMEM((PAD + (n_blocks + 1) * band * examples, LANES), jnp.float32),
            pltpu.SemaphoreType.DMA((2, PARTS)),
            pltpu.SemaphoreType.DMA,
            pltpu.SemaphoreType.DMA,
            pltpu.SMEM((n_kept // LANES, LANES), jnp.int32),
            pltpu.SMEM((n_blocks + GROUP * bands + 2 * AT_ONCE,), jnp.int32),
        ],
        compiler_params=pltpu.CompilerParams(vmem_limit_bytes=VMEM_LIMIT),
    )(
        *(
            pltpu.with_memory_space_constraint(value, pltpu.HBM)
            for value in (
                pattern, x_acts, delta, cols.reshape(-1, LANES), sign_rows,
                col_signs.reshape(-1, LANES),
            )
        )
    )


def per_device(x_acts, delta, pattern, row_signs, col_signs, cols):
    rows = delta.shape[2]
    feat = lax.axis_size("feat")
    me = lax.axis_index("feat")
    if rows % LANES == 0:
        sign_rows = row_signs.reshape(-1, LANES)
    else:
        sign_rows = lax.dynamic_slice_in_dim(row_signs, me * rows, rows, 0)[None]

    mine, other = sketch(x_acts, delta, pattern, sign_rows, col_signs, cols)

    bits = max(feat - 1, 0).bit_length()
    mine = mine + partner(other, "feat", 0)
    for bit in range(1, bits):
        mine = mine + partner(mine, "feat", bit)
    back = partner(mine, "feat", 0)
    low = me % 2 == 0
    return jnp.concatenate([jnp.where(low, mine, back), jnp.where(low, back, mine)], axis=1)


def solution(mesh):
    placed = (P("grp", None, None), P("grp", None, "feat"), P(), P(), P(), P())
    return jax.shard_map(
        per_device, mesh=mesh, in_specs=placed, out_specs=P("grp", None), check_vma=False
    )
```

```python
import functools
import math

import jax
import jax.numpy as jnp
from jax import lax
from jax.experimental import pallas as pl
from jax.experimental.pallas import tpu as pltpu
from jax.sharding import PartitionSpec as P

BLK = 128
LANES = 128
SUBLANES = 8
AT_ONCE = 8
GROUP = 4
PAD = 8
VMEM_LIMIT = 44 * 2**20


def partner(value, axis, apart):
    mask = 2**apart
    pairs = [(source, source ^ mask) for source in range(lax.axis_size(axis))]
    return lax.ppermute(value, axis, pairs)


def parity(ids):
    for shift in (8, 4, 2, 1):
        ids = ids ^ (ids >> shift)
    return ids & 1


def iota(shape, dim):
    return lax.broadcasted_iota(jnp.int32, shape, dim)


def aligned(index, unit):
    return pl.multiple_of(index * unit, unit)


def butterfly(tiles):
    half = 1
    while half < len(tiles):
        tiles = [
            tiles[q] + tiles[q + half] if q & half == 0 else tiles[q - half] - tiles[q]
            for q in range(len(tiles))
        ]
        half *= 2
    return tiles


def sketch_kernel(
    scale, pattern_hbm, x_hbm, d_hbm, cols_hbm, rows_hbm, signs_hbm, mine_ref, other_ref,
    pattern, cols_ref, rows_ref, signs_ref, small_sem, x_ref, d_ref, dt_ref, had_ref, flip_even, flip_odd, idx_ref, signed_ref, t_ref, x_sem, d_sem, idx_sem, idx_smem, listed,
):
    examples, tokens, width = x_hbm.shape
    rows = d_hbm.shape[2]
    n_cols = width // LANES
    bands = dt_ref.shape[0] // examples
    band = rows // bands
    n_blocks = bands * n_cols
    block_rows = band * examples
    n_kept = cols_ref.shape[0] * LANES
    per_vreg = SUBLANES // examples
    me = lax.axis_index("feat")
    first = me * rows // BLK

    def x_copy(example, q):
        slot = example % 2
        lanes = pl.ds(aligned(q, LANES), LANES)
        return pltpu.make_async_copy(
            x_hbm.at[example, :, lanes], x_ref.at[slot, q], x_sem.at[slot, q]
        )

    def each_used(act):
        def body(q, carry):
            used = pattern[first, q]
            for b in range(1, bands):
                used = used | pattern[first + b, q]

            @pl.when(used != 0)
            def _():
                act(q)

            return carry

        lax.fori_loop(0, n_cols, body, 0)

    small = [
        pltpu.make_async_copy(source, target, small_sem.at[i])
        for i, (source, target) in enumerate(
            (
                (cols_hbm, cols_ref),
                (pattern_hbm, pattern),
                (rows_hbm, rows_ref),
                (signs_hbm, signs_ref),
            )
        )
    ]
    for copy in small:
        copy.start()
    d_copy = pltpu.make_async_copy(d_hbm, d_ref, d_sem)
    d_copy.start()
    for q in range(n_cols):
        x_copy(0, q).start()

    had_ref[...] = (1 - 2 * parity(iota((band, band), 0) & iota((band, band), 1))).astype(
        jnp.bfloat16
    )
    bits = (iota((SUBLANES, LANES), 1) >> iota((SUBLANES, LANES), 0) & 1).astype(jnp.bfloat16)
    for copy in small:
        copy.wait()

    cols = cols_ref[...]
    kept_row, kept_col = cols // width, cols % width
    local = kept_row % rows
    block = local // band * n_cols + kept_col // LANES
    place = iota(cols.shape, 0) % per_vreg
    idx_ref[...] = PAD + (block * band + local % band) * examples - place * examples

    def flips(group, flip_ref):
        digits = []
        for p in range(per_vreg):
            lane = cols_ref[pl.ds(group * per_vreg + p, 1), :] % LANES
            digits.append((lane >> iota((SUBLANES, LANES), 0) & 1).astype(jnp.bfloat16))
        shared = lax.dot_general(
            jnp.concatenate(digits, axis=1),
            bits,
            (((0,), (0,)), ((), ())),
            preferred_element_type=jnp.float32,
        )
        odd = (shared.astype(jnp.int32) & 1).astype(jnp.float32)
        flip_ref[...] = 1.0 - 2.0 * odd


    count = AT_ONCE
    for b in range(bands):
        for q in range(n_cols):
            listed[count] = b * n_cols + q
            count = count + pattern[first + b, q]
        for extra in range(GROUP):
            listed[count + extra] = n_blocks
        count = (count + GROUP - 1) // GROUP * GROUP
    for extra in range(AT_ONCE):
        listed[count + extra] = n_blocks
    n_steps = jnp.maximum((count - 1) // AT_ONCE, 1)
    for i in range(AT_ONCE):
        listed[i] = listed[n_steps * AT_ONCE + i]

    idx_copy = pltpu.make_async_copy(idx_ref, idx_smem, idx_sem)
    idx_copy.start()

    for b in range(bands):
        def clear(q, carry):
            @pl.when(pattern[first + b, q] == 0)
            def _():
                start = PAD + (b * n_cols + q) * block_rows
                here = pl.ds(pl.multiple_of(start, SUBLANES), block_rows)
                t_ref[here, :] = jnp.zeros((block_rows, LANES), jnp.float32)

            return carry

        lax.fori_loop(0, n_cols, clear, 0)

    if rows % LANES == 0:
        row_flip = jnp.concatenate(
            [rows_ref[pl.ds(me * (rows // LANES) + i, 1), :] for i in range(rows // LANES)],
            axis=1,
        ).astype(jnp.bfloat16)
    else:
        row_flip = rows_ref[...].astype(jnp.bfloat16)
    d_copy.wait()
    for example in range(examples):
        turned = (d_ref[example] * row_flip).T
        for b in range(bands):
            dt_ref[example * bands + b] = turned[b * band : (b + 1) * band, :]

    def finish(at, example):
        sums = jnp.dot(had_ref[...], signed_ref[...], preferred_element_type=jnp.float32)
        for i in range(AT_ONCE):
            start = PAD + listed[at + i] * block_rows + example
            t_ref[pl.ds(start, band, stride=examples), :] = sums[:, i * LANES : (i + 1) * LANES]

    def one_example(example, carry):
        @pl.when(example == 0)
        def _():
            for q in range(n_cols):
                x_copy(0, q).wait()

        @pl.when(example > 0)
        def _():
            each_used(lambda q: x_copy(example, q).wait())

        @pl.when(example + 1 < examples)
        def _():
            each_used(lambda q: x_copy(example + 1, q).start())

        def some_blocks(s, carry):
            finish(s * AT_ONCE, jnp.where(s == 0, jnp.maximum(example - 1, 0), example))
            for g in range(AT_ONCE // GROUP):
                ids = [listed[(s + 1) * AT_ONCE + g * GROUP + k] for k in range(GROUP)]
                acts = [x_ref[example % 2, i % n_cols] for i in ids]
                flip = [signs_ref[pl.ds(i % n_cols, 1), :] for i in ids]
                grad = jnp.dot(
                    dt_ref[example * bands + ids[0] // n_cols % bands],
                    jnp.concatenate(acts, axis=1),
                    preferred_element_type=jnp.float32,
                )
                flip = jnp.concatenate(flip, axis=1).astype(jnp.float32)
                here = slice(g * GROUP * LANES, (g + 1) * GROUP * LANES)
                signed_ref[:, here] = (grad * flip).astype(jnp.bfloat16)
            return carry

        lax.fori_loop(0, n_steps, some_blocks, 0)

        return carry

    lax.fori_loop(0, examples, one_example, 0)
    finish(n_steps * AT_ONCE, examples - 1)

    def across(r, carry):
        def here(i):
            start = PAD + i * block_rows + r * SUBLANES
            return pl.ds(pl.multiple_of(start, SUBLANES), SUBLANES)

        for b in range(bands):
            tiles = butterfly([t_ref[here(b * n_cols + q), :] for q in range(n_cols)])
            if b % 2 == 0:
                for q in range(n_cols):
                    t_ref[here(b * n_cols + q), :] = tiles[q]
            else:
                for q in range(n_cols):
                    low = t_ref[here((b - 1) * n_cols + q), :]
                    t_ref[here((b - 1) * n_cols + q), :] = low + tiles[q]
                    t_ref[here(b * n_cols + q), :] = low - tiles[q]
        return carry

    lax.fori_loop(0, block_rows // SUBLANES, across, 0)

    idx_copy.wait()
    lane = iota((SUBLANES, LANES), 1)
    spot = iota((SUBLANES, LANES), 0) // examples
    n_groups = n_kept // LANES // per_vreg
    half = n_groups // 2

    def one_group(group, out_ref, at, flip_ref):
        found = jnp.zeros((SUBLANES, LANES), jnp.float32)
        for u in range(LANES):
            term = None
            for p in range(per_vreg):
                tile = t_ref[pl.ds(idx_smem[group * per_vreg + p, u], SUBLANES), :]
                tile = tile * flip_ref[pl.ds(p * LANES + u, SUBLANES, stride=0), :]
                term = tile if p == 0 else jnp.where(spot == p, tile, term)
            total = jnp.sum(term, axis=1, keepdims=True)
            found = jnp.where(lane == u, total, found)
        for p in range(per_vreg):
            top = cols_ref[pl.ds(group * per_vreg + p, 1), :] // width // rows
            factor = (1 - 2 * parity(top & me)).astype(jnp.float32) * scale
            there = pl.ds(aligned(at * per_vreg + p, LANES), LANES)
            out_ref[:, there] = found[p * examples : (p + 1) * examples] * factor

    def sample(out_ref, base):
        def body(i, carry):
            group = base + 2 * i
            flips(group + 1, flip_odd)
            one_group(group, out_ref, 2 * i, flip_even)
            flips(lax.rem(group + 2, n_groups), flip_even)
            one_group(group + 1, out_ref, 2 * i + 1, flip_odd)
            return carry

        lax.fori_loop(0, half // 2, body, 0)

    theirs = (1 - me % 2) * half
    flips(theirs, flip_even)
    sample(other_ref, theirs)
    sample(mine_ref, me % 2 * half)


def sketch(x_acts, delta, pattern, sign_rows, col_signs, cols):
    examples, tokens, width = x_acts.shape
    rows = delta.shape[2]
    n_kept = cols.shape[0]
    bands = max(rows // BLK, 1)
    band = rows // bands
    n_blocks = bands * width // LANES
    per_vreg = SUBLANES // examples
    hbm = pl.BlockSpec(memory_space=pltpu.HBM)
    vmem = pl.BlockSpec(memory_space=pltpu.VMEM)
    scale = 1.0 / (tokens * math.sqrt(n_kept))
    part = jax.ShapeDtypeStruct((examples, n_kept // 2), jnp.float32)
    return pl.pallas_call(
        functools.partial(sketch_kernel, scale),
        out_shape=(part, part),
        in_specs=[hbm] * 6,
        out_specs=(vmem, vmem),
        scratch_shapes=[
            pltpu.SMEM(pattern.shape, jnp.int32),
            pltpu.VMEM((n_kept // LANES, LANES), jnp.int32),
            pltpu.VMEM(sign_rows.shape, jnp.int32),
            pltpu.VMEM((width // LANES, LANES), jnp.int32),
            pltpu.SemaphoreType.DMA((4,)),
            pltpu.VMEM((2, width // LANES, tokens, LANES), jnp.bfloat16),
            pltpu.VMEM((examples, tokens, rows), jnp.bfloat16),
            pltpu.VMEM((examples * bands, band, tokens), jnp.bfloat16),
            pltpu.VMEM((band, band), jnp.bfloat16),
            pltpu.VMEM((per_vreg * LANES, LANES), jnp.float32),
            pltpu.VMEM((per_vreg * LANES, LANES), jnp.float32),
            pltpu.VMEM((n_kept // LANES, LANES), jnp.int32),
            pltpu.VMEM((band, AT_ONCE * LANES), jnp.bfloat16),
            pltpu.VMEM((PAD + (n_blocks + 1) * band * examples, LANES), jnp.float32),
            pltpu.SemaphoreType.DMA((2, width // LANES)),
            pltpu.SemaphoreType.DMA,
            pltpu.SemaphoreType.DMA,
            pltpu.SMEM((n_kept // LANES, LANES), jnp.int32),
            pltpu.SMEM((n_blocks + GROUP * bands + 2 * AT_ONCE,), jnp.int32),
        ],
        compiler_params=pltpu.CompilerParams(vmem_limit_bytes=VMEM_LIMIT),
    )(
        *(
            pltpu.with_memory_space_constraint(value, pltpu.HBM)
            for value in (
                pattern, x_acts, delta, cols.reshape(-1, LANES), sign_rows,
                col_signs.reshape(-1, LANES),
            )
        )
    )


def per_device(x_acts, delta, pattern, row_signs, col_signs, cols):
    rows = delta.shape[2]
    feat = lax.axis_size("feat")
    me = lax.axis_index("feat")
    if rows % LANES == 0:
        sign_rows = row_signs.reshape(-1, LANES)
    else:
        sign_rows = lax.dynamic_slice_in_dim(row_signs, me * rows, rows, 0)[None]

    mine, other = sketch(x_acts, delta, pattern, sign_rows, col_signs, cols)

    bits = max(feat - 1, 0).bit_length()
    mine = mine + partner(other, "feat", 0)
    for bit in range(1, bits):
        mine = mine + partner(mine, "feat", bit)
    back = partner(mine, "feat", 0)
    low = me % 2 == 0
    return jnp.concatenate([jnp.where(low, mine, back), jnp.where(low, back, mine)], axis=1)


def solution(mesh):
    placed = (P("grp", None, None), P("grp", None, "feat"), P(), P(), P(), P())
    return jax.shard_map(
        per_device, mesh=mesh, in_specs=placed, out_specs=P("grp", None), check_vma=False
    )
```

```python
import functools
import math

import jax
import jax.numpy as jnp
from jax import lax
from jax.experimental import pallas as pl
from jax.experimental.pallas import tpu as pltpu
from jax.sharding import PartitionSpec as P

BLK = 128
LANES = 128
SUBLANES = 8
AT_ONCE = 8
GROUP = 4
RADIX = 16
PAD = 8
VMEM_LIMIT = 44 * 2**20


def partner(value, axis, apart):
    mask = 2**apart
    pairs = [(source, source ^ mask) for source in range(lax.axis_size(axis))]
    return lax.ppermute(value, axis, pairs)


def parity(ids):
    for shift in (8, 4, 2, 1):
        ids = ids ^ (ids >> shift)
    return ids & 1


def iota(shape, dim):
    return lax.broadcasted_iota(jnp.int32, shape, dim)


def aligned(index, unit):
    return pl.multiple_of(index * unit, unit)


def butterfly(tiles):
    half = 1
    while half < len(tiles):
        tiles = [
            tiles[q] + tiles[q + half] if q & half == 0 else tiles[q - half] - tiles[q]
            for q in range(len(tiles))
        ]
        half *= 2
    return tiles


def sketch_kernel(
    scale, pattern_hbm, x_hbm, d_hbm, cols_hbm, rows_hbm, signs_hbm, mine_ref, other_ref,
    pattern, cols_ref, rows_ref, signs_ref, small_sem, x_ref, d_ref, dt_ref, had_ref, flip_even, flip_odd, idx_ref, signed_ref, t_ref, x_sem, d_sem, idx_sem, idx_smem, listed, left_out,
):
    examples, tokens, width = x_hbm.shape
    rows = d_hbm.shape[2]
    n_cols = width // LANES
    bands = dt_ref.shape[0] // examples
    band = rows // bands
    n_blocks = bands * n_cols
    block_rows = band * examples
    n_kept = cols_ref.shape[0] * LANES
    per_vreg = SUBLANES // examples
    me = lax.axis_index("feat")
    first = me * rows // BLK

    def x_copy(example, q):
        slot = example % 2
        lanes = pl.ds(aligned(q, LANES), LANES)
        return pltpu.make_async_copy(
            x_hbm.at[example, :, lanes], x_ref.at[slot, q], x_sem.at[slot, q]
        )

    def each_used(act, begin, end):
        def body(q, carry):
            used = pattern[first, q]
            for b in range(1, bands):
                used = used | pattern[first + b, q]

            @pl.when(used != 0)
            def _():
                act(q)

            return carry

        lax.fori_loop(begin, end, body, 0)

    def start_used(example, begin, end):
        @pl.when(example < examples)
        def _():
            each_used(lambda q: x_copy(example, q).start(), begin, end)

    ahead = n_cols // 2
    small = [
        pltpu.make_async_copy(source, target, small_sem.at[i])
        for i, (source, target) in enumerate(
            (
                (cols_hbm, cols_ref),
                (pattern_hbm, pattern),
                (rows_hbm, rows_ref),
                (signs_hbm, signs_ref),
            )
        )
    ]
    for copy in small:
        copy.start()
    d_copy = pltpu.make_async_copy(d_hbm, d_ref, d_sem)
    d_copy.start()
    for q in range(n_cols):
        x_copy(0, q).start()

    had_ref[...] = (1 - 2 * parity(iota((band, band), 0) & iota((band, band), 1))).astype(
        jnp.bfloat16
    )
    bits = (iota((SUBLANES, LANES), 1) >> iota((SUBLANES, LANES), 0) & 1).astype(jnp.bfloat16)
    for copy in small:
        copy.wait()

    cols = cols_ref[...]
    kept_row, kept_col = cols // width, cols % width
    local = kept_row % rows
    block = local // band * n_cols + kept_col // LANES
    place = iota(cols.shape, 0) % per_vreg
    idx_ref[...] = PAD + (block * band + local % band) * examples - place * examples

    def flips(group, flip_ref):
        digits = []
        for p in range(per_vreg):
            lane = cols_ref[pl.ds(group * per_vreg + p, 1), :] % LANES
            digits.append((lane >> iota((SUBLANES, LANES), 0) & 1).astype(jnp.bfloat16))
        shared = lax.dot_general(
            jnp.concatenate(digits, axis=1),
            bits,
            (((0,), (0,)), ((), ())),
            preferred_element_type=jnp.float32,
        )
        odd = (shared.astype(jnp.int32) & 1).astype(jnp.float32)
        flip_ref[...] = 1.0 - 2.0 * odd


    count = AT_ONCE
    for b in range(bands):
        for q in range(n_cols):
            listed[count] = b * n_cols + q
            count = count + pattern[first + b, q]
        for extra in range(GROUP):
            listed[count + extra] = n_blocks
        count = (count + GROUP - 1) // GROUP * GROUP
    for extra in range(AT_ONCE):
        listed[count + extra] = n_blocks
    n_steps = jnp.maximum((count - 1) // AT_ONCE, 1)
    for i in range(AT_ONCE):
        listed[i] = listed[n_steps * AT_ONCE + i]

    idx_copy = pltpu.make_async_copy(idx_ref, idx_smem, idx_sem)
    idx_copy.start()
    start_used(1, 0, ahead)

    spare = 0
    for i in range(n_blocks):
        left_out[spare] = i
        spare = spare + 1 - pattern[first + i // n_cols, i % n_cols]

    def clear(i, carry):
        start = PAD + left_out[i] * block_rows
        here = pl.ds(pl.multiple_of(start, SUBLANES), block_rows)
        t_ref[here, :] = jnp.zeros((block_rows, LANES), jnp.float32)
        return carry

    lax.fori_loop(0, spare, clear, 0)

    if rows % LANES == 0:
        row_flip = jnp.concatenate(
            [rows_ref[pl.ds(me * (rows // LANES) + i, 1), :] for i in range(rows // LANES)],
            axis=1,
        ).astype(jnp.bfloat16)
    else:
        row_flip = rows_ref[...].astype(jnp.bfloat16)
    d_copy.wait()
    for example in range(examples):
        turned = (d_ref[example] * row_flip).T
        for b in range(bands):
            dt_ref[example * bands + b] = turned[b * band : (b + 1) * band, :]

    def finish(at, example):
        sums = jnp.dot(had_ref[...], signed_ref[...], preferred_element_type=jnp.float32)
        for i in range(AT_ONCE):
            start = PAD + listed[at + i] * block_rows + example
            t_ref[pl.ds(start, band, stride=examples), :] = sums[:, i * LANES : (i + 1) * LANES]

    def one_example(example, carry):
        @pl.when(example == 0)
        def _():
            for q in range(n_cols):
                x_copy(0, q).wait()

        @pl.when(example > 0)
        def _():
            start_used(example + 1, 0, ahead)
            each_used(lambda q: x_copy(example, q).wait(), 0, n_cols)

        start_used(example + 1, ahead, n_cols)

        def some_blocks(s, carry):
            finish(s * AT_ONCE, jnp.where(s == 0, jnp.maximum(example - 1, 0), example))
            for g in range(AT_ONCE // GROUP):
                ids = [listed[(s + 1) * AT_ONCE + g * GROUP + k] for k in range(GROUP)]
                acts = [x_ref[example % 2, i % n_cols] for i in ids]
                flip = [signs_ref[pl.ds(i % n_cols, 1), :] for i in ids]
                grad = jnp.dot(
                    dt_ref[example * bands + ids[0] // n_cols % bands],
                    jnp.concatenate(acts, axis=1),
                    preferred_element_type=jnp.float32,
                )
                flip = jnp.concatenate(flip, axis=1).astype(jnp.float32)
                here = slice(g * GROUP * LANES, (g + 1) * GROUP * LANES)
                signed_ref[:, here] = (grad * flip).astype(jnp.bfloat16)
            return carry

        lax.fori_loop(0, n_steps, some_blocks, 0)

        return carry

    lax.fori_loop(0, examples, one_example, 0)
    finish(n_steps * AT_ONCE, examples - 1)

    def across(r, carry):
        def here(i):
            start = PAD + i * block_rows + r * SUBLANES
            return pl.ds(pl.multiple_of(start, SUBLANES), SUBLANES)

        done = 1
        while done < n_blocks:
            radix = min(RADIX, n_blocks // done)
            for lead in range(0, n_blocks, done * radix):
                for low in range(done):
                    ids = [lead + low + k * done for k in range(radix)]
                    tiles = butterfly([t_ref[here(i), :] for i in ids])
                    for i, tile in zip(ids, tiles):
                        t_ref[here(i), :] = tile
            done *= radix
        return carry

    lax.fori_loop(0, block_rows // SUBLANES, across, 0)

    idx_copy.wait()
    lane = iota((SUBLANES, LANES), 1)
    spot = iota((SUBLANES, LANES), 0) // examples
    n_groups = n_kept // LANES // per_vreg
    half = n_groups // 2

    def one_group(group, out_ref, at, flip_ref):
        found = jnp.zeros((SUBLANES, LANES), jnp.float32)
        for u in range(LANES):
            term = None
            for p in range(per_vreg):
                tile = t_ref[pl.ds(idx_smem[group * per_vreg + p, u], SUBLANES), :]
                tile = tile * flip_ref[pl.ds(p * LANES + u, SUBLANES, stride=0), :]
                term = tile if p == 0 else jnp.where(spot == p, tile, term)
            total = jnp.sum(term, axis=1, keepdims=True)
            found = jnp.where(lane == u, total, found)
        for p in range(per_vreg):
            top = cols_ref[pl.ds(group * per_vreg + p, 1), :] // width // rows
            factor = (1 - 2 * parity(top & me)).astype(jnp.float32) * scale
            there = pl.ds(aligned(at * per_vreg + p, LANES), LANES)
            out_ref[:, there] = found[p * examples : (p + 1) * examples] * factor

    def sample(out_ref, base):
        def body(i, carry):
            group = base + 2 * i
            flips(group + 1, flip_odd)
            one_group(group, out_ref, 2 * i, flip_even)
            flips(lax.rem(group + 2, n_groups), flip_even)
            one_group(group + 1, out_ref, 2 * i + 1, flip_odd)
            return carry

        lax.fori_loop(0, half // 2, body, 0)

    theirs = (1 - me % 2) * half
    flips(theirs, flip_even)
    sample(other_ref, theirs)
    sample(mine_ref, me % 2 * half)


def sketch(x_acts, delta, pattern, sign_rows, col_signs, cols):
    examples, tokens, width = x_acts.shape
    rows = delta.shape[2]
    n_kept = cols.shape[0]
    bands = max(rows // BLK, 1)
    band = rows // bands
    n_blocks = bands * width // LANES
    per_vreg = SUBLANES // examples
    hbm = pl.BlockSpec(memory_space=pltpu.HBM)
    vmem = pl.BlockSpec(memory_space=pltpu.VMEM)
    scale = 1.0 / (tokens * math.sqrt(n_kept))
    part = jax.ShapeDtypeStruct((examples, n_kept // 2), jnp.float32)
    return pl.pallas_call(
        functools.partial(sketch_kernel, scale),
        out_shape=(part, part),
        in_specs=[hbm] * 6,
        out_specs=(vmem, vmem),
        scratch_shapes=[
            pltpu.SMEM(pattern.shape, jnp.int32),
            pltpu.VMEM((n_kept // LANES, LANES), jnp.int32),
            pltpu.VMEM(sign_rows.shape, jnp.int32),
            pltpu.VMEM((width // LANES, LANES), jnp.int32),
            pltpu.SemaphoreType.DMA((4,)),
            pltpu.VMEM((2, width // LANES, tokens, LANES), jnp.bfloat16),
            pltpu.VMEM((examples, tokens, rows), jnp.bfloat16),
            pltpu.VMEM((examples * bands, band, tokens), jnp.bfloat16),
            pltpu.VMEM((band, band), jnp.bfloat16),
            pltpu.VMEM((per_vreg * LANES, LANES), jnp.float32),
            pltpu.VMEM((per_vreg * LANES, LANES), jnp.float32),
            pltpu.VMEM((n_kept // LANES, LANES), jnp.int32),
            pltpu.VMEM((band, AT_ONCE * LANES), jnp.bfloat16),
            pltpu.VMEM((PAD + (n_blocks + 1) * band * examples, LANES), jnp.float32),
            pltpu.SemaphoreType.DMA((2, width // LANES)),
            pltpu.SemaphoreType.DMA,
            pltpu.SemaphoreType.DMA,
            pltpu.SMEM((n_kept // LANES, LANES), jnp.int32),
            pltpu.SMEM((n_blocks + GROUP * bands + 2 * AT_ONCE,), jnp.int32),
            pltpu.SMEM((n_blocks,), jnp.int32),
        ],
        compiler_params=pltpu.CompilerParams(vmem_limit_bytes=VMEM_LIMIT),
    )(
        *(
            pltpu.with_memory_space_constraint(value, pltpu.HBM)
            for value in (
                pattern, x_acts, delta, cols.reshape(-1, LANES), sign_rows,
                col_signs.reshape(-1, LANES),
            )
        )
    )


def per_device(x_acts, delta, pattern, row_signs, col_signs, cols):
    rows = delta.shape[2]
    feat = lax.axis_size("feat")
    me = lax.axis_index("feat")
    if rows % LANES == 0:
        sign_rows = row_signs.reshape(-1, LANES)
    else:
        sign_rows = lax.dynamic_slice_in_dim(row_signs, me * rows, rows, 0)[None]

    mine, other = sketch(x_acts, delta, pattern, sign_rows, col_signs, cols)

    bits = max(feat - 1, 0).bit_length()
    mine = mine + partner(other, "feat", 0)
    for bit in range(1, bits):
        mine = mine + partner(mine, "feat", bit)
    back = partner(mine, "feat", 0)
    low = me % 2 == 0
    return jnp.concatenate([jnp.where(low, mine, back), jnp.where(low, back, mine)], axis=1)


def solution(mesh):
    placed = (P("grp", None, None), P("grp", None, "feat"), P(), P(), P(), P())
    return jax.shard_map(
        per_device, mesh=mesh, in_specs=placed, out_specs=P("grp", None), check_vma=False
    )
```
